256 devices in a mesh: ctx: 64 (over y, z, core), head: 4 (over x).
Axes of the slice: x: 4, y: 4, z: 8, core: 2. Of those that a mesh axis runs over, the one named last changes fastest.
Arguments:
- tokens: bfloat16 [8192, 2048], P('ctx'), may hold values from -6 to 6
- grad_out: bfloat16 [8192, 2048], P('ctx'), may hold values from -6 to 6
- expert_ids: int32 [8192, 8], P('ctx'), may hold values from 0 to 127, all different within a row; in each aligned block of 128 rows (0 to 127, 128 to 255, ...) at most 10 rows name the same one
- gate_probs: bfloat16 [8192, 8], P('ctx'), may hold values from 0.029907227 to 0.3984375
- w_gate: bfloat16 [128, 768, 2048], P('ctx', 'head'), may hold values from -0.125 to 0.125
- w_up: bfloat16 [128, 768, 2048], P('ctx', 'head'), may hold values from -0.125 to 0.125
- w_down: bfloat16 [128, 768, 2048], P('ctx', 'head'), may hold values from -0.21875 to 0.21875
- query_rows: bfloat16 [8192, 4096], P('ctx', 'head'), may hold values from -4.5 to 4.5, as said below
- key_rows: bfloat16 [8192, 512], P('ctx', 'head'), may hold values from -4.5 to 4.5, as said below
- value_rows: bfloat16 [8192, 512], P('ctx', 'head'), may hold values from -6 to 6
- attn_out: bfloat16 [8192, 4096], P('ctx', 'head'), may hold values from -6 to 6
- grad_attn: bfloat16 [8192, 4096], P('ctx', 'head'), may hold values from -6 to 6
- segment_ids: int32 [8192], replicated, may hold values from 0 to 63, never falling along the last dimension, each value on 1 to 384 neighbouring positions
Outputs:
- grad_tokens: bfloat16 [8192, 2048], P('ctx')
- grad_gate: bfloat16 [128, 768, 2048], P('ctx', 'head')
- grad_up: bfloat16 [128, 768, 2048], P('ctx', 'head')
- grad_down: bfloat16 [128, 768, 2048], P('ctx', 'head')
- grad_query: bfloat16 [8192, 4096], P('ctx', 'head')
- grad_key: bfloat16 [8192, 512], P('ctx', 'head')
- grad_value: bfloat16 [8192, 512], P('ctx', 'head')
The draws below stay inside these ranges and needn't reach their ends.
Inputs may be any that keep to these rules, and one draw needn't show every extreme that they name: `expert_ids`: each row names different experts; among the 128 tokens of one index of ctx no expert is named more than 10 times, a bound that some block reaches. `segment_ids`: ids never fall; a document has at most 384 positions, and one has exactly that many. `query_rows`: entries stay within the range. `key_rows`: entries stay within the range.
All inputs are finite; a program needn't handle non-finite values.
Results may differ from the reference program's by a relative error of at most 0.0057.
Values may be sent and summed in bfloat16 or wider, within the bound.
No kernel may reach another device: no remote copies, remote signals or barrier semaphores. Data moves between devices by JAX's collectives and lax.ppermute only.
A program may use at most 128 MiB of HBM per device.

```python
import math
import jax
import jax.numpy as jnp
import numpy as np
from jax import lax

D = 2048
FF = 768
TOPK = 8
HQ = 32
KVH = 4
HD = 128
TOK_DEV = 128
ATT_DEV = 128
REACH = 3
EXPERTS = 128
CAP = 10
TOKENS = 8192
ATT_TOK = 8192
N_CTX = 64


def drawn_pair(base_key):
    folded = jax.random.fold_in(base_key, 4242)
    subkeys = jax.random.split(folded, 2)
    query_draw = jnp.clip(jax.random.normal(subkeys[0], (ATT_TOK, HQ * HD), jnp.float32), -4.5, 4.5)
    key_draw = jnp.clip(jax.random.normal(subkeys[1], (ATT_TOK, KVH * HD), jnp.float32), -4.5, 4.5)
    return (query_draw, key_draw)


def draw_query_rows(key, part):
    return drawn_pair(key)[0].astype(jnp.bfloat16)


def draw_key_rows(key, part):
    return drawn_pair(key)[1].astype(jnp.bfloat16)


def levels(key, dims, shards, low, top_value):
    gain, own = 1.0, jax.random.fold_in(key, 6)
    for axis_at, blocks in shards:
        heights = jnp.exp(jax.random.uniform(jax.random.fold_in(own, axis_at), (blocks,), jnp.float32, low / len(shards), top_value / len(shards)))
        gain = gain * jnp.repeat(heights, dims[axis_at] // blocks).reshape([-1 if axis == axis_at else 1 for axis in range(len(dims))])
    return gain


def profile(count, total, most, lean):
    portions = [(1 << 20) // math.isqrt(grade ** lean) + 1 for grade in range(2, count + 1)]
    surplus, counts = total - most - (count - 1), [1] * (count - 1)
    while surplus > 0:
        movable = [i for i in range(count - 1) if counts[i] < most]
        mass, remaining = sum([portions[i] for i in movable]), surplus
        for i in movable:
            more = min(most - counts[i], max(1, remaining * portions[i] // mass), surplus)
            counts[i] = counts[i] + more
            surplus = surplus - more
    return np.array([most] + counts)


def uneven_parts(own_key, number_of, total, most, lean):
    if number_of == 2:
        one = jax.random.randint(own_key, (), max(1, total - most), min(most, total - 1) + 1)
        return jnp.stack([one, total - one])
    lengths = jnp.asarray(profile(number_of, total, most, lean), jnp.int32)
    couples = (number_of - 1) // 2
    donor, receiver = lengths[1:1 + 2 * couples:2], lengths[2:2 + 2 * couples:2]
    margin = jnp.minimum(donor - 1, most - receiver)
    passed = jax.random.randint(jax.random.fold_in(own_key, 1), (couples,), 0, 1 << 20) % (margin + 1)
    lengths = lengths.at[1:1 + 2 * couples:2].set(donor - passed).at[2:2 + 2 * couples:2].set(receiver + passed)
    return lengths[jax.random.permutation(jax.random.fold_in(own_key, 2), number_of)]


def assign_block(stream_key, own, number, rows, amount, top, bound, lean):
    ranking = jax.random.permutation(stream_key, amount)
    heavy_load, usual = shares(amount, rows * top, bound, lean, True), shares(amount, rows * top, bound, lean, False)
    places = jnp.arange(amount)

    def named(lengths, turn):
        used = int((lengths > 0).sum())
        fixed = max(1, used // 4)
        passed = fixed + (places - fixed + turn * (used - fixed)) % max(1, amount - fixed)
        return jnp.zeros((amount,), jnp.int32).at[ranking[jnp.where(places < fixed, places, passed)]].set(jnp.asarray(lengths, jnp.int32))

    lengths = jnp.where(number % 4 == 0, named(heavy_load, number // 4), named(usual, number - number // 4 - 1))
    mixed = jax.random.permutation(jax.random.fold_in(own, 3), amount)
    source_of, receiver = mixed[0:amount // 2 * 2:2], mixed[1:amount // 2 * 2:2]
    margin = jnp.minimum(lengths[source_of] - 1, bound - lengths[receiver]) // 2
    margin = jnp.where((source_of == ranking[0]) | (receiver == ranking[0]) | (lengths[receiver] == 0), 0, jnp.maximum(margin, 0))
    passed = jax.random.randint(jax.random.fold_in(own, 4), (amount // 2,), 0, 1 << 20) % (margin + 1)
    lengths = lengths.at[source_of].add(-passed).at[receiver].add(passed)
    members = jnp.searchsorted(jnp.cumsum(lengths), jnp.arange(rows * top), side="right").astype(jnp.int32)
    table = members.reshape(top, rows).T
    table = table[jax.random.permutation(jax.random.fold_in(own, 1), rows)]
    turn = jax.random.randint(jax.random.fold_in(own, 2), (rows, 1), 0, top)
    return jnp.take_along_axis(table, (jnp.arange(top)[None, :] + turn) % top, axis=1)


def shares(number_of, total, most, lean, full):
    loads = [(1 << 20) // math.isqrt(grade ** lean) + 1 for grade in range(1, number_of + 1)]
    largest = most if full else min(most, max(-(-total // number_of), total * loads[0] // sum(loads)))
    least = 1 if total - largest >= number_of - 1 else 0
    holding, surplus = [largest] + [least] * (number_of - 1), total - largest - least * (number_of - 1)
    while surplus > 0:
        candidates = [i for i in range(1, number_of) if holding[i] < largest] or [i for i in range(1, number_of) if holding[i] < most]
        whole, left = sum([loads[i] for i in candidates]), surplus
        for i in candidates:
            extra = min(most - holding[i], max(1, left * loads[i] // whole), surplus)
            holding[i] = holding[i] + extra
            surplus = surplus - extra
    return np.array(holding)


def gaussian(rng, dims, scale, bound, cuts=(), kind=jnp.bfloat16):
    factor_of = levels(rng, dims, cuts, -0.22, 0.18) if cuts else 1.0
    values = jax.random.normal(rng, dims, jnp.float32) * scale * factor_of
    return jnp.minimum(jnp.maximum(values, -bound), bound).astype(kind)


def setup_inputs(seed: int = 0) -> dict:
    arg_keys = jax.random.split(jax.random.key(seed), 14)
    tokens = gaussian(arg_keys[0], (TOKENS, D), 1.0, 6.0, ((0, 64),))
    grad_out = gaussian(arg_keys[1], (TOKENS, D), 1.0, 6.0, ((0, 64),))
    expert_ids_keys = jax.random.split(jax.random.fold_in(arg_keys[2], 1), TOKENS // TOK_DEV)
    expert_ids_turns = jax.random.permutation(jax.random.fold_in(arg_keys[2], 3), TOKENS // TOK_DEV)
    expert_ids = jax.vmap(lambda own, number: assign_block(jax.random.fold_in(arg_keys[2], 2), own, number, TOK_DEV, EXPERTS, TOPK, CAP, 2))(expert_ids_keys, expert_ids_turns).reshape((TOKENS, TOPK))
    gate_probs = jnp.clip(jnp.exp(math.log(0.3984375) - 2.5894505 * jax.random.uniform(arg_keys[3], (TOKENS, TOPK), jnp.float32) ** levels(arg_keys[3], (TOKENS, TOPK), ((0, 64),), -0.2, 0.2)), 0.029907227, 0.3984375).astype(jnp.bfloat16)
    w_gate = gaussian(arg_keys[4], (EXPERTS, FF, D), D ** -0.5, 0.125, ((0, 64), (1, 4)))
    w_up = gaussian(arg_keys[5], (EXPERTS, FF, D), D ** -0.5, 0.125, ((0, 64), (1, 4)))
    w_down = gaussian(arg_keys[6], (EXPERTS, FF, D), FF ** -0.5, 0.21875, ((0, 64), (1, 4)))
    query_rows = draw_query_rows(jax.random.fold_in(arg_keys[13], 71), 0)
    key_rows = draw_key_rows(jax.random.fold_in(arg_keys[13], 71), 0)
    value_rows = gaussian(arg_keys[9], (ATT_TOK, KVH * HD), 1.0, 6.0, ((0, 64), (1, 4)))
    attn_out = gaussian(arg_keys[10], (ATT_TOK, HQ * HD), 1.0, 6.0, ((0, 64), (1, 4)))
    grad_attn = gaussian(arg_keys[11], (ATT_TOK, HQ * HD), 1.0, 6.0, ((0, 64), (1, 4)))
    segment_ids = jnp.searchsorted(jnp.cumsum(uneven_parts(arg_keys[12], N_CTX, ATT_TOK, REACH * ATT_DEV, 2)), jnp.arange(ATT_TOK), side="right").astype(jnp.int32)
    return dict(tokens=tokens, grad_out=grad_out, expert_ids=expert_ids, gate_probs=gate_probs, w_gate=w_gate, w_up=w_up, w_down=w_down, query_rows=query_rows, key_rows=key_rows, value_rows=value_rows, attn_out=attn_out, grad_attn=grad_attn, segment_ids=segment_ids)


def expert_terms(rows_in, grad_rows, gate_mat, up_mat, down_mat):
    gate_pre = jnp.dot(rows_in, gate_mat.T, preferred_element_type=jnp.float32)
    up_pre = jnp.dot(rows_in, up_mat.T, preferred_element_type=jnp.float32)
    sigmoid_gate = jax.nn.sigmoid(gate_pre)
    active = gate_pre * sigmoid_gate
    hidden = (active * up_pre).astype(jnp.bfloat16)
    hidden_grad = jnp.dot(grad_rows, down_mat.T, preferred_element_type=jnp.float32)
    gate_grad = (hidden_grad * up_pre * sigmoid_gate * (1.0 + gate_pre * (1.0 - sigmoid_gate))).astype(jnp.bfloat16)
    up_grad = (hidden_grad * active).astype(jnp.bfloat16)
    returned = jnp.dot(gate_grad, gate_mat, preferred_element_type=jnp.float32) + jnp.dot(up_grad, up_mat, preferred_element_type=jnp.float32)
    gate_part = jnp.dot(gate_grad.T, rows_in, preferred_element_type=jnp.float32).astype(jnp.bfloat16)
    up_part = jnp.dot(up_grad.T, rows_in, preferred_element_type=jnp.float32).astype(jnp.bfloat16)
    down_part = jnp.dot(hidden.T, grad_rows, preferred_element_type=jnp.float32).astype(jnp.bfloat16)
    return returned, gate_part, up_part, down_part


def moe_backward(tokens, grad_out, expert_ids, gate_probs, w_gate, w_up, w_down):
    pair_count = TOKENS * TOPK
    slot_total = N_CTX * CAP
    flat_expert = expert_ids.reshape(pair_count)
    padded_tokens = jnp.concatenate([tokens, jnp.zeros((1, D), tokens.dtype)], axis=0)
    padded_grad = jnp.concatenate([grad_out, jnp.zeros((1, D), grad_out.dtype)], axis=0)
    padded_probs = jnp.concatenate([gate_probs.reshape(pair_count).astype(jnp.float32), jnp.zeros((1,), jnp.float32)])

    def expert_step(accumulated, expert):
        pair_list = jnp.nonzero(flat_expert == expert, size=slot_total, fill_value=pair_count)[0].astype(jnp.int32)
        token_list = (pair_list // TOPK).astype(jnp.int32)
        rows_in = padded_tokens[token_list]
        grad_rows = (padded_probs[pair_list][:, None] * padded_grad[token_list].astype(jnp.float32)).astype(jnp.bfloat16)
        returned, gate_part, up_part, down_part = expert_terms(rows_in, grad_rows, w_gate[expert], w_up[expert], w_down[expert])
        accumulated = accumulated.at[token_list].add(returned)
        return accumulated, (gate_part, up_part, down_part)

    start_sum = jnp.zeros((TOKENS + 1, D), jnp.float32)
    summed, grads = lax.scan(expert_step, start_sum, jnp.arange(EXPERTS, dtype=jnp.int32))
    return summed[:TOKENS].astype(jnp.bfloat16), grads[0], grads[1], grads[2]


def attention_backward(query_rows, key_rows, value_rows, attn_out, grad_attn, segment_ids):
    group_size = HQ // KVH
    window = (REACH + 1) * ATT_DEV
    pad_rows = REACH * ATT_DEV
    score_scale = HD ** -0.5
    padded_key = jnp.concatenate([jnp.zeros((pad_rows, KVH * HD), key_rows.dtype), key_rows], axis=0)
    padded_value = jnp.concatenate([jnp.zeros((pad_rows, KVH * HD), value_rows.dtype), value_rows], axis=0)
    padded_segment = jnp.concatenate([jnp.full((pad_rows,), -1, jnp.int32), segment_ids.astype(jnp.int32)])
    positions = jnp.arange(ATT_TOK + pad_rows, dtype=jnp.int32) - pad_rows

    def block_step(carried, block_index):
        key_accum, value_accum = carried
        row_start = (block_index * ATT_DEV).astype(jnp.int32)
        query_heads = lax.dynamic_slice_in_dim(query_rows, row_start, ATT_DEV, 0).astype(jnp.float32).reshape(ATT_DEV, KVH, group_size, HD)
        out_heads = lax.dynamic_slice_in_dim(attn_out, row_start, ATT_DEV, 0).astype(jnp.float32).reshape(ATT_DEV, KVH, group_size, HD)
        grad_heads = lax.dynamic_slice_in_dim(grad_attn, row_start, ATT_DEV, 0).astype(jnp.float32).reshape(ATT_DEV, KVH, group_size, HD)
        window_key = lax.dynamic_slice_in_dim(padded_key, row_start, window, 0).astype(jnp.float32).reshape(window, KVH, HD)
        window_value = lax.dynamic_slice_in_dim(padded_value, row_start, window, 0).astype(jnp.float32).reshape(window, KVH, HD)
        query_pos = row_start + jnp.arange(ATT_DEV, dtype=jnp.int32)
        key_pos = lax.dynamic_slice_in_dim(positions, row_start, window, 0)
        query_seg = lax.dynamic_slice_in_dim(segment_ids.astype(jnp.int32), row_start, ATT_DEV, 0)
        key_seg = lax.dynamic_slice_in_dim(padded_segment, row_start, window, 0)
        visible = (key_pos[None, :] <= query_pos[:, None]) & (key_seg[None, :] == query_seg[:, None])
        scores = jnp.einsum("ajgd,tjd->jgat", query_heads, window_key) * score_scale
        row_peak = jnp.max(jnp.where(visible, scores, -jnp.inf), axis=-1, keepdims=True)
        weights_exp = jnp.exp(jnp.where(visible, scores - row_peak, -jnp.inf))
        probs = weights_exp / jnp.sum(weights_exp, axis=-1, keepdims=True)
        row_delta = jnp.einsum("ajgd,ajgd->jga", grad_heads, out_heads)
        prob_grad = jnp.einsum("ajgd,tjd->jgat", grad_heads, window_value)
        score_grad = (probs * (prob_grad - row_delta[..., None])).astype(jnp.bfloat16)
        probs_low = probs.astype(jnp.bfloat16)
        grad_query = (score_scale * jnp.einsum("jgat,tjd->ajgd", score_grad.astype(jnp.float32), window_key)).astype(jnp.bfloat16)
        key_terms = (score_scale * jnp.einsum("jgat,ajgd->tjd", score_grad.astype(jnp.float32), query_heads)).reshape(window, KVH * HD)
        value_terms = jnp.einsum("jgat,ajgd->tjd", probs_low.astype(jnp.float32), grad_heads).reshape(window, KVH * HD)
        key_accum = lax.dynamic_update_slice_in_dim(key_accum, lax.dynamic_slice_in_dim(key_accum, row_start, window, 0) + key_terms, row_start, 0)
        value_accum = lax.dynamic_update_slice_in_dim(value_accum, lax.dynamic_slice_in_dim(value_accum, row_start, window, 0) + value_terms, row_start, 0)
        return (key_accum, value_accum), grad_query.reshape(ATT_DEV, HQ * HD)

    start_key = jnp.zeros((ATT_TOK + pad_rows, KVH * HD), jnp.float32)
    start_value = jnp.zeros((ATT_TOK + pad_rows, KVH * HD), jnp.float32)
    carried, blocks = lax.scan(block_step, (start_key, start_value), jnp.arange(N_CTX, dtype=jnp.int32))
    grad_query = blocks.reshape(ATT_TOK, HQ * HD)
    return grad_query, carried[0][pad_rows:].astype(jnp.bfloat16), carried[1][pad_rows:].astype(jnp.bfloat16)


def reference(tokens, grad_out, expert_ids, gate_probs, w_gate, w_up, w_down, query_rows, key_rows, value_rows, attn_out, grad_attn, segment_ids):
    grad_tokens, grad_gate, grad_up, grad_down = moe_backward(tokens, grad_out, expert_ids, gate_probs, w_gate, w_up, w_down)
    grad_query, grad_key, grad_value = attention_backward(query_rows, key_rows, value_rows, attn_out, grad_attn, segment_ids)
    return (grad_tokens, grad_gate, grad_up, grad_down, grad_query, grad_key, grad_value)
```

```python
import functools

import jax
import jax.numpy as jnp
import numpy as np
from jax import lax
from jax.experimental import pallas as pl
from jax.experimental.pallas import tpu as pltpu
from jax.sharding import PartitionSpec as P

HQ = 32
KVH = 4
HD = 128
REACH = 3
CAP = 10
LOCAL = 2
SLOTS = LOCAL * CAP
GROUP = 2 * SLOTS
BF = jnp.bfloat16
F32 = jnp.float32


def passed_along(block, axis, distance):
    devices = range(lax.axis_size(axis))
    route = [(i - distance, i) for i in devices if i - distance in devices]
    return lax.ppermute(block, axis, route)


def turned(block, distance):
    count = lax.axis_size("head")
    return lax.ppermute(block, "head", [(i, (i + distance) % count) for i in range(count)])


def spec():
    return pl.BlockSpec(memory_space=pltpu.VMEM)


def dot_nt(a, b):
    return lax.dot_general(a, b, (((1,), (1,)), ((), ())), preferred_element_type=F32)


def dot_nn(a, b):
    return lax.dot_general(a, b, (((1,), (0,)), ((), ())), preferred_element_type=F32)


def dot_tn(a, b):
    return lax.dot_general(a, b, (((0,), (0,)), ((), ())), preferred_element_type=F32)


def column_block(shape, offset):
    block = shape[:-1] + (shape[-1] // 4,)
    lead = (0,) * (len(shape) - 1)
    return pl.BlockSpec(block, lambda i, head, lead=lead, offset=offset: lead + ((head[0] + offset) % 4,))


def whole(shape):
    zeros = (0,) * len(shape)
    return pl.BlockSpec(shape, lambda i, head, zeros=zeros: zeros)


def call(kernel, head, ins, outs, scratch=()):
    arrays = [a for a, _ in ins]
    return pl.pallas_call(
        kernel,
        grid_spec=pltpu.PrefetchScalarGridSpec(
            num_scalar_prefetch=1,
            grid=(1,),
            in_specs=[s for _, s in ins],
            out_specs=[s for _, s in outs],
            scratch_shapes=list(scratch),
        ),
        out_shape=[o for o, _ in outs],
        compiler_params=pltpu.CompilerParams(vmem_limit_bytes=56 << 20),
    )(head, *arrays)


def full(a):
    return (a, whole(a.shape))


def out(shape, dtype):
    return (jax.ShapeDtypeStruct(shape, dtype), whole(shape))


def route_kernel(head, ids, probs, pattern, tok, rows_ref, pick_ref, scaled_ref, rank_s, prob_s):
    experts, count = rank_s.shape
    where_e = lax.broadcasted_iota(jnp.int32, (experts, count), 0)
    hits = jnp.zeros((experts, count), F32)
    chance = jnp.zeros((experts, count), F32)
    for k in range(ids.shape[0]):
        hit = ids[k : k + 1, :] == where_e
        hits = jnp.where(hit, 1.0, hits)
        chance = jnp.where(hit, probs[k : k + 1, :], chance)
    first = lax.broadcasted_iota(jnp.int32, (count, count), 0)
    second = lax.broadcasted_iota(jnp.int32, (count, count), 1)
    before = jnp.where(first < second, 1.0, 0.0).astype(BF)
    rank = dot_nn(hits.astype(BF), before)
    rank_s[...] = jnp.where(hits > 0.0, rank, -1.0)
    prob_s[...] = chance
    which = pattern[0]
    place = pattern[1]
    lower = pattern[2]

    def step(i, carry):
        base = i * (2 * LOCAL)
        value = rank_s[pl.ds(base, 1), :]
        weight = prob_s[pl.ds(base, 1), :]
        for j in range(1, 2 * LOCAL):
            mine = which == j
            value = jnp.where(mine, rank_s[pl.ds(base + j, 1), :], value)
            weight = jnp.where(mine, prob_s[pl.ds(base + j, 1), :], weight)
        match = jnp.where(value == place, 1.0, 0.0)
        weight = match * weight
        at = pl.multiple_of(i * 2 * GROUP, 2 * GROUP)
        zero = jnp.zeros_like(match)
        in_low = lower > 0.0
        pick_ref[pl.ds(at, 2 * GROUP), 0:count] = jnp.where(in_low, match, zero).astype(BF)
        pick_ref[pl.ds(at, 2 * GROUP), count : 2 * count] = jnp.where(in_low, zero, match).astype(BF)
        scaled_ref[pl.ds(at, 2 * GROUP), 0:count] = jnp.where(in_low, weight, zero).astype(BF)
        scaled_ref[pl.ds(at, 2 * GROUP), count : 2 * count] = jnp.where(in_low, zero, weight).astype(BF)
        return carry

    lax.fori_loop(0, experts // (2 * LOCAL), step, 0)
    half = tok.shape[1] // 2
    stacked = jnp.concatenate([tok[:, :half], tok[:, half:]], axis=0)
    rows_ref[...] = dot_nn(pick_ref[...], stacked).astype(BF)


def select_kernel(head, scaled, tok, rows_ref):
    half = tok.shape[1] // 2
    stacked = jnp.concatenate([tok[:, :half], tok[:, half:]], axis=0)
    rows_ref[...] = dot_nn(scaled[...], stacked).astype(BF)


def pattern_table(count):
    r = np.arange(2 * GROUP)
    which = (r // GROUP) * LOCAL + (r % SLOTS) // CAP
    place = r % CAP
    lower = (r % GROUP) < SLOTS
    table = np.stack([which, place, lower]).astype(np.float32)
    return jnp.asarray(np.repeat(table[:, :, None], count, axis=2))


def untangle_kernel(head, recv, low_ref, high_ref, wide):
    sources = recv.shape[0] // GROUP
    half = recv.shape[1]
    lanes = wide[0].shape[1]
    for p in range(half // lanes):
        wide[p][...] = recv[:, p * lanes : (p + 1) * lanes].astype(F32)
    for e, ref in ((0, low_ref), (1, high_ref)):
        for c in range(CAP):
            for part in range(2):
                for p in range(half // lanes):
                    rows = wide[p][pl.ds(part * SLOTS + e * CAP + c, sources, stride=GROUP), :]
                    col = part * half + p * lanes
                    ref[c * sources : (c + 1) * sources, col : col + lanes] = rows.astype(BF)


def tangle_kernel(head, own, left_a, left_b, right_a, right_b, send_ref, wide):
    rows = own.shape[0] // 2
    sources = rows // CAP
    half = own.shape[1] // 2
    lanes = wide[0].shape[1]
    for e, (a, b) in ((0, (left_b, right_a)), (1, (left_a, right_b))):
        for c in range(CAP):
            for part in range(2):
                for p in range(half // lanes):
                    col = part * half + p * lanes
                    at = c * sources
                    total = (
                        own[e * rows + at : e * rows + at + sources, col : col + lanes]
                        + a[at : at + sources, col : col + lanes].astype(F32)
                        + b[at : at + sources, col : col + lanes].astype(F32)
                    )
                    wide[p][pl.ds(part * SLOTS + e * CAP + c, sources, stride=GROUP), :] = total
    for p in range(half // lanes):
        send_ref[:, p * lanes : (p + 1) * lanes] = wide[p][...].astype(BF)


def pre_kernel(head, *refs):
    blocks, gates, ups = refs[0:8], refs[8:12], refs[12:16]
    act_ref, slope_ref, hidden_ref = refs[16:]
    for e in range(LOCAL):
        rows = blocks[e].shape[0]
        gate = dot_nt(blocks[e][...], gates[0][e])
        up = dot_nt(blocks[e][...], ups[0][e])
        for q in range(1, 4):
            gate = gate + dot_nt(blocks[2 * q + e][...], gates[q][e])
            up = up + dot_nt(blocks[2 * q + e][...], ups[q][e])
        sig = jax.nn.sigmoid(gate)
        active = gate * sig
        at = pl.ds(e * rows, rows)
        act_ref[at, :] = active
        slope_ref[at, :] = up * sig * (1.0 + gate * (1.0 - sig))
        hidden_ref[at, :] = (active * up).astype(BF)


def grad_kernel(head, *refs):
    blocks, downs = refs[0:8], refs[8:12]
    act, slope, gate_far, up_far = refs[12:16]
    gg_ref, ug_ref, far_low, far_high = refs[16:]
    for e, far in ((0, far_low), (1, far_high)):
        rows = blocks[e].shape[0]
        got = dot_nt(blocks[e][...], downs[0][e])
        for q in range(1, 4):
            got = got + dot_nt(blocks[2 * q + e][...], downs[q][e])
        at = pl.ds(e * rows, rows)
        gg = (got * slope[at, :]).astype(BF)
        ug = (got * act[at, :]).astype(BF)
        gg_ref[at, :] = gg
        ug_ref[at, :] = ug
        far[...] = (dot_nn(gg, gate_far[e]) + dot_nn(ug, up_far[e])).astype(BF)


def back_kernel(head, gg, ug, gate_p, up_p, gate_m, up_m, gate_o, up_o, p0, p1, m0, m1, own):
    rows = gg.shape[0] // 2
    low, high = pl.ds(0, rows), pl.ds(rows, rows)
    p1[...] = (dot_nn(gg[high, :], gate_p[1]) + dot_nn(ug[high, :], up_p[1])).astype(BF)
    m0[...] = (dot_nn(gg[low, :], gate_m[0]) + dot_nn(ug[low, :], up_m[0])).astype(BF)
    p0[...] = dot_nn(gg[low, :], gate_p[0]) + dot_nn(ug[low, :], up_p[0])
    m1[...] = dot_nn(gg[high, :], gate_m[1]) + dot_nn(ug[high, :], up_m[1])
    own[low, :] = dot_nn(gg[low, :], gate_o[0]) + dot_nn(ug[low, :], up_o[0])
    own[high, :] = dot_nn(gg[high, :], gate_o[1]) + dot_nn(ug[high, :], up_o[1])


def weight_kernel(head, *refs):
    blocks = refs[0:8]
    sides = len(refs[8:]) // 2
    lefts, results = refs[8 : 8 + sides], refs[8 + sides :]
    width = blocks[0].shape[1]
    offsets = (0, 3, 1, 2)
    for q in range(4):
        col = pl.multiple_of(((head[0] + offsets[q]) % 4) * width, width)
        for e in range(LOCAL):
            rows = blocks[e].shape[0]
            data = blocks[2 * q + e][...]
            for left, result in zip(lefts, results):
                part = dot_tn(left[pl.ds(e * rows, rows), :], data)
                result[e, :, pl.ds(col, width)] = part.astype(BF)


def round_ring(low, high):
    right_low = turned(low, 1)
    left_high = turned(high, -1)
    right_high = turned(high, 1)
    left_low = turned(low, -1)
    far_low = turned(right_low, 1)
    far_high = turned(left_high, -1)
    return [low, high, right_low, right_high, left_low, left_high, far_low, far_high]


def dispatch(send, head, count, lanes):
    half = send.shape[1]
    recv = lax.all_to_all(
        send.reshape(count, GROUP, half), "ctx", split_axis=0, concat_axis=0, tiled=True
    ).reshape(count * GROUP, half)
    low, high = call(
        untangle_kernel,
        head,
        [full(recv)],
        [out((count * CAP, 2 * half), BF), out((count * CAP, 2 * half), BF)],
        [[pltpu.VMEM((count * GROUP, lanes), F32) for _ in range(half // lanes)]],
    )
    return round_ring(low, high)


def attention(query_rows, window_kv, attn_out, grad_attn, segment_ids, kv_width):
    att_rows = query_rows.shape[0]
    kv_local = kv_width // HD
    group_size = HQ // KVH
    window = (REACH + 1) * att_rows
    score_scale = HD ** (-0.5)
    ctx_index = lax.axis_index("ctx")
    window_key = window_kv[:, :kv_width].reshape(window, kv_local, HD)
    window_value = window_kv[:, kv_width:].reshape(window, kv_local, HD)
    query_pos = ctx_index * att_rows + jnp.arange(att_rows, dtype=jnp.int32)
    key_pos = (ctx_index - REACH) * att_rows + jnp.arange(window, dtype=jnp.int32)
    padded_segment = jnp.concatenate([jnp.full((REACH * att_rows,), -1, jnp.int32), segment_ids])
    key_seg = lax.dynamic_slice_in_dim(padded_segment, ctx_index * att_rows, window, 0)
    query_seg = lax.dynamic_slice_in_dim(segment_ids, ctx_index * att_rows, att_rows, 0)
    visible = (key_pos[None, :] <= query_pos[:, None]) & (key_seg[None, :] == query_seg[:, None])
    query_heads = query_rows.reshape(att_rows, kv_local, group_size, HD)
    out_heads = attn_out.reshape(att_rows, kv_local, group_size, HD)
    grad_heads = grad_attn.reshape(att_rows, kv_local, group_size, HD)
    scores = (
        jnp.einsum("ajgd,tjd->jgat", query_heads, window_key, preferred_element_type=F32)
        * score_scale
    )
    row_peak = jnp.max(jnp.where(visible, scores, -jnp.inf), axis=-1, keepdims=True)
    weights_exp = jnp.exp(jnp.where(visible, scores - row_peak, -jnp.inf))
    probs = weights_exp / jnp.sum(weights_exp, axis=-1, keepdims=True)
    row_delta = jnp.einsum("ajgd,ajgd->jga", grad_heads, out_heads, preferred_element_type=F32)
    prob_grad = jnp.einsum("ajgd,tjd->jgat", grad_heads, window_value, preferred_element_type=F32)
    score_grad = (probs * (prob_grad - row_delta[..., None])).astype(BF)
    probs_low = probs.astype(BF)
    grad_query = (
        (score_scale * jnp.einsum("jgat,tjd->ajgd", score_grad, window_key, preferred_element_type=F32))
        .astype(BF)
        .reshape(att_rows, -1)
    )
    key_terms = (
        score_scale
        * jnp.einsum("jgat,ajgd->tjd", score_grad, query_heads, preferred_element_type=F32)
    ).reshape(window, kv_width)
    value_terms = jnp.einsum(
        "jgat,ajgd->tjd", probs_low, grad_heads, preferred_element_type=F32
    ).reshape(window, kv_width)
    return grad_query, jnp.concatenate([key_terms, value_terms], axis=1)


def body(
    tokens,
    grad_out,
    expert_ids,
    gate_probs,
    w_gate,
    w_up,
    w_down,
    query_rows,
    key_rows,
    value_rows,
    attn_out,
    grad_attn,
    segment_ids,
):
    tok_count, width = tokens.shape
    count = lax.axis_size("ctx")
    quarter = width // 4
    half = quarter // 2
    lanes = min(half, 128)
    hidden_local = w_gate.shape[1]
    head = lax.axis_index("head").astype(jnp.int32).reshape(1)
    experts = count * LOCAL
    slots = count * GROUP
    rows = count * CAP
    kv_width = key_rows.shape[1]
    att_rows = query_rows.shape[0]

    kv = jnp.concatenate([key_rows, value_rows], axis=1)
    kv_blocks = [passed_along(kv, "ctx", distance) for distance in range(REACH, 0, -1)]

    send_rows, pick, scaled = call(
        route_kernel,
        head,
        [
            full(expert_ids.T),
            full(gate_probs.T.astype(F32)),
            full(pattern_table(tok_count)),
            (tokens, column_block(tokens.shape, 0)),
        ],
        [out((slots, half), BF), out((slots, 2 * tok_count), BF), out((slots, 2 * tok_count), BF)],
        [pltpu.VMEM((experts, tok_count), F32), pltpu.VMEM((experts, tok_count), F32)],
    )
    send_rows, kv_blocks = lax.optimization_barrier((send_rows, kv_blocks))
    (send_grads,) = call(
        select_kernel,
        head,
        [full(scaled), (grad_out, column_block(grad_out.shape, 0))],
        [out((slots, half), BF)],
    )
    row_blocks = dispatch(send_rows, head, count, lanes)
    grad_blocks = dispatch(send_grads, head, count, lanes)

    gate_at = lambda offset: (w_gate, column_block(w_gate.shape, offset))
    up_at = lambda offset: (w_up, column_block(w_up.shape, offset))
    down_at = lambda offset: (w_down, column_block(w_down.shape, offset))
    order = (0, 3, 1, 2)
    act, slope, hidden = call(
        pre_kernel,
        head,
        [full(b) for b in row_blocks] + [gate_at(o) for o in order] + [up_at(o) for o in order],
        [
            out((2 * rows, hidden_local), F32),
            out((2 * rows, hidden_local), F32),
            out((2 * rows, hidden_local), BF),
        ],
    )
    gg, ug, far_low, far_high = call(
        grad_kernel,
        head,
        [full(b) for b in grad_blocks]
        + [down_at(o) for o in order]
        + [full(act), full(slope), gate_at(2), up_at(2)],
        [
            out((2 * rows, hidden_local), BF),
            out((2 * rows, hidden_local), BF),
            out((rows, quarter), BF),
            out((rows, quarter), BF),
        ],
    )
    near_low = turned(far_low, 1)
    near_high = turned(far_high, -1)
    p0, p1, m0, m1, own = call(
        back_kernel,
        head,
        [full(gg), full(ug), gate_at(1), up_at(1), gate_at(3), up_at(3), gate_at(0), up_at(0)],
        [
            out((rows, quarter), F32),
            out((rows, quarter), BF),
            out((rows, quarter), BF),
            out((rows, quarter), F32),
            out((2 * rows, quarter), F32),
        ],
    )
    left_a = turned(p1, 1)
    right_a = turned(m0, -1)
    left_b = turned((p0 + near_low.astype(F32)).astype(BF), 1)
    right_b = turned((m1 + near_high.astype(F32)).astype(BF), -1)
    (send_back,) = call(
        tangle_kernel,
        head,
        [full(own), full(left_a), full(left_b), full(right_a), full(right_b)],
        [out((slots, half), BF)],
        [[pltpu.VMEM((slots, lanes), F32) for _ in range(half // lanes)]],
    )
    returned = lax.all_to_all(
        send_back.reshape(count, GROUP, half), "ctx", split_axis=0, concat_axis=0, tiled=True
    ).reshape(slots, half)
    summed = dot_tn(pick, returned)
    token_part = jnp.concatenate([summed[:tok_count], summed[tok_count:]], axis=1).astype(BF)
    grad_tokens = lax.all_gather(token_part, "head", axis=1, tiled=True)

    weight_out = out(w_gate.shape, BF)
    grad_gate, grad_up = call(
        weight_kernel,
        head,
        [full(b) for b in row_blocks] + [full(gg), full(ug)],
        [weight_out, weight_out],
    )
    (grad_down,) = call(
        weight_kernel, head, [full(b) for b in grad_blocks] + [full(hidden)], [weight_out]
    )

    grad_query, terms = attention(
        query_rows,
        jnp.concatenate(kv_blocks + [kv], axis=0),
        attn_out,
        grad_attn,
        segment_ids,
        kv_width,
    )
    total = terms[REACH * att_rows :]
    for distance in range(1, REACH + 1):
        offset = (REACH - distance) * att_rows
        total = total + passed_along(terms[offset : offset + att_rows], "ctx", -distance)
    total = total.astype(BF)
    return (
        grad_tokens,
        grad_gate,
        grad_up,
        grad_down,
        grad_query,
        total[:, :kv_width],
        total[:, kv_width:],
    )


def solution(mesh):
    placed = (
        P("ctx", None),
        P("ctx", None),
        P("ctx", None),
        P("ctx", None),
        P("ctx", "head", None),
        P("ctx", "head", None),
        P("ctx", "head", None),
        P("ctx", "head"),
        P("ctx", "head"),
        P("ctx", "head"),
        P("ctx", "head"),
        P("ctx", "head"),
        P(),
    )
    return jax.shard_map(
        body,
        mesh=mesh,
        in_specs=placed,
        out_specs=(
            P("ctx", None),
            P("ctx", "head", None),
            P("ctx", "head", None),
            P("ctx", "head", None),
            P("ctx", "head"),
            P("ctx", "head"),
            P("ctx", "head"),
        ),
        check_vma=False,
    )
```

```python
import jax
import jax.numpy as jnp
import numpy as np
from jax import lax
from jax.experimental import pallas as pl
from jax.experimental.pallas import tpu as pltpu
from jax.sharding import PartitionSpec as P


HQ = 32
KVH = 4
HD = 128
REACH = 3
CAP = 10
LOCAL = 2
SLOTS = LOCAL * CAP
GROUP = 2 * SLOTS
BF = jnp.bfloat16
F32 = jnp.float32


def passed_along(block, axis, distance):
    devices = range(lax.axis_size(axis))
    route = [(i - distance, i) for i in devices if i - distance in devices]
    return lax.ppermute(block, axis, route)


def turned(block, distance):
    count = lax.axis_size("head")
    return lax.ppermute(block, "head", [(i, (i + distance) % count) for i in range(count)])


def dot_nt(a, b):
    return lax.dot_general(a, b, (((1,), (1,)), ((), ())), preferred_element_type=F32)


def dot_nn(a, b):
    return lax.dot_general(a, b, (((1,), (0,)), ((), ())), preferred_element_type=F32)


def dot_tn(a, b):
    return lax.dot_general(a, b, (((0,), (0,)), ((), ())), preferred_element_type=F32)


def column_block(shape, offset):
    block = shape[:-1] + (shape[-1] // 4,)
    lead = (0,) * (len(shape) - 1)
    return pl.BlockSpec(block, lambda i, head, lead=lead, offset=offset: lead + ((head[0] + offset) % 4,))


def whole(shape):
    zeros = (0,) * len(shape)
    return pl.BlockSpec(shape, lambda i, head, zeros=zeros: zeros)


def call(kernel, head, ins, outs, scratch=()):
    return launched(kernel, head, ins, outs, scratch)


def launched(kernel, head, ins, outs, scratch):
    arrays = [a for a, _ in ins]
    return pl.pallas_call(
        kernel,
        grid_spec=pltpu.PrefetchScalarGridSpec(
            num_scalar_prefetch=1,
            grid=(1,),
            in_specs=[s for _, s in ins],
            out_specs=[s for _, s in outs],
            scratch_shapes=list(scratch),
        ),
        out_shape=[o for o, _ in outs],
        compiler_params=pltpu.CompilerParams(vmem_limit_bytes=56 << 20),
    )(head, *arrays)


def full(a):
    return (a, whole(a.shape))


def out(shape, dtype):
    return (jax.ShapeDtypeStruct(shape, dtype), whole(shape))


def route_kernel(head, ids, probs, pattern, tok, rows_ref, pick_ref, scaled_ref, rank_s, prob_s):
    experts, count = rank_s.shape
    where_e = lax.broadcasted_iota(jnp.int32, (experts, count), 0)
    hits = jnp.zeros((experts, count), F32)
    chance = jnp.zeros((experts, count), F32)
    weights = probs[...].astype(F32)
    for k in range(ids.shape[0]):
        hit = ids[k : k + 1, :] == where_e
        hits = jnp.where(hit, 1.0, hits)
        chance = jnp.where(hit, weights[k : k + 1, :], chance)
    first = lax.broadcasted_iota(jnp.int32, (count, count), 0)
    second = lax.broadcasted_iota(jnp.int32, (count, count), 1)
    before = jnp.where(first < second, 1.0, 0.0).astype(BF)
    rank = dot_nn(hits.astype(BF), before)
    rank_s[...] = jnp.where(hits > 0.0, rank, -1.0)
    prob_s[...] = chance
    which = pattern[0]
    place = pattern[1]
    lower = pattern[2]

    def step(i, carry):
        base = i * (2 * LOCAL)
        value = rank_s[pl.ds(base, 1), :]
        weight = prob_s[pl.ds(base, 1), :]
        for j in range(1, 2 * LOCAL):
            mine = which == j
            value = jnp.where(mine, rank_s[pl.ds(base + j, 1), :], value)
            weight = jnp.where(mine, prob_s[pl.ds(base + j, 1), :], weight)
        match = jnp.where(value == place, 1.0, 0.0)
        weight = match * weight
        at = pl.multiple_of(i * 2 * GROUP, 2 * GROUP)
        zero = jnp.zeros_like(match)
        in_low = lower > 0.0
        pick_ref[pl.ds(at, 2 * GROUP), 0:count] = jnp.where(in_low, match, zero).astype(BF)
        pick_ref[pl.ds(at, 2 * GROUP), count : 2 * count] = jnp.where(in_low, zero, match).astype(BF)
        scaled_ref[pl.ds(at, 2 * GROUP), 0:count] = jnp.where(in_low, weight, zero).astype(BF)
        scaled_ref[pl.ds(at, 2 * GROUP), count : 2 * count] = jnp.where(in_low, zero, weight).astype(BF)
        return carry

    lax.fori_loop(0, experts // (2 * LOCAL), step, 0)
    half = tok.shape[1] // 2
    stacked = jnp.concatenate([tok[:, :half], tok[:, half:]], axis=0)
    rows_ref[...] = dot_nn(pick_ref[...], stacked).astype(BF)


def select_kernel(head, scaled, tok, rows_ref):
    half = tok.shape[1] // 2
    stacked = jnp.concatenate([tok[:, :half], tok[:, half:]], axis=0)
    rows_ref[...] = dot_nn(scaled[...], stacked).astype(BF)


def pattern_table(count):
    r = np.arange(2 * GROUP)
    which = (r // GROUP) * LOCAL + (r % SLOTS) // CAP
    place = r % CAP
    lower = (r % GROUP) < SLOTS
    table = np.stack([which, place, lower]).astype(np.float32)
    return jnp.asarray(np.repeat(table[:, :, None], count, axis=2))


def untangle_kernel(head, recv, low_ref, high_ref, wide):
    sources = recv.shape[0] // GROUP
    half = recv.shape[1]
    lanes = wide[0].shape[1]
    for p in range(half // lanes):
        wide[p][...] = recv[:, p * lanes : (p + 1) * lanes].astype(F32)
    for e, ref in ((0, low_ref), (1, high_ref)):
        for c in range(CAP):
            for part in range(2):
                for p in range(half // lanes):
                    rows = wide[p][pl.ds(part * SLOTS + e * CAP + c, sources, stride=GROUP), :]
                    col = part * half + p * lanes
                    ref[c * sources : (c + 1) * sources, col : col + lanes] = rows.astype(BF)


def tangle_kernel(head, own, left_a, left_b, right_a, right_b, send_ref, wide):
    rows = own.shape[0] // 2
    sources = rows // CAP
    half = own.shape[1] // 2
    lanes = wide[0].shape[1]
    for e, (a, b) in ((0, (left_b, right_a)), (1, (left_a, right_b))):
        for c in range(CAP):
            for part in range(2):
                for p in range(half // lanes):
                    col = part * half + p * lanes
                    at = c * sources
                    total = (
                        own[e * rows + at : e * rows + at + sources, col : col + lanes]
                        + a[at : at + sources, col : col + lanes].astype(F32)
                        + b[at : at + sources, col : col + lanes].astype(F32)
                    )
                    wide[p][pl.ds(part * SLOTS + e * CAP + c, sources, stride=GROUP), :] = total
    for p in range(half // lanes):
        send_ref[:, p * lanes : (p + 1) * lanes] = wide[p][...].astype(BF)


def pre_kernel(head, *refs):
    blocks, gates, ups = refs[0:8], refs[8:12], refs[12:16]
    act_ref, slope_ref, hidden_ref = refs[16:]
    for e in range(LOCAL):
        rows = blocks[e].shape[0]
        gate = dot_nt(blocks[e][...], gates[0][e])
        up = dot_nt(blocks[e][...], ups[0][e])
        for q in range(1, 4):
            gate = gate + dot_nt(blocks[2 * q + e][...], gates[q][e])
            up = up + dot_nt(blocks[2 * q + e][...], ups[q][e])
        sig = jax.nn.sigmoid(gate)
        active = gate * sig
        at = pl.ds(e * rows, rows)
        act_ref[at, :] = active
        slope_ref[at, :] = up * sig * (1.0 + gate * (1.0 - sig))
        hidden_ref[at, :] = (active * up).astype(BF)


def near_kernel(head, *refs):
    blocks, downs, got_ref = refs[0:6], refs[6:9], refs[9]
    for e in range(LOCAL):
        rows = blocks[e].shape[0]
        got = dot_nt(blocks[e][...], downs[0][e])
        for q in range(1, 3):
            got = got + dot_nt(blocks[2 * q + e][...], downs[q][e])
        got_ref[pl.ds(e * rows, rows), :] = got


def grad_kernel(head, low, high, down, got_near, act, slope, gate_far, up_far, *outs):
    gg_ref, ug_ref, far_low, far_high = outs
    for e, block, far in ((0, low, far_low), (1, high, far_high)):
        rows = block.shape[0]
        at = pl.ds(e * rows, rows)
        got = got_near[at, :] + dot_nt(block[...], down[e])
        gg = (got * slope[at, :]).astype(BF)
        ug = (got * act[at, :]).astype(BF)
        gg_ref[at, :] = gg
        ug_ref[at, :] = ug
        far[...] = (dot_nn(gg, gate_far[e]) + dot_nn(ug, up_far[e])).astype(BF)


def back_kernel(head, gg, ug, gate_p, up_p, gate_m, up_m, gate_o, up_o, p0, p1, m0, m1, own):
    rows = gg.shape[0] // 2
    low, high = pl.ds(0, rows), pl.ds(rows, rows)
    p1[...] = (dot_nn(gg[high, :], gate_p[1]) + dot_nn(ug[high, :], up_p[1])).astype(BF)
    m0[...] = (dot_nn(gg[low, :], gate_m[0]) + dot_nn(ug[low, :], up_m[0])).astype(BF)
    p0[...] = dot_nn(gg[low, :], gate_p[0]) + dot_nn(ug[low, :], up_p[0])
    m1[...] = dot_nn(gg[high, :], gate_m[1]) + dot_nn(ug[high, :], up_m[1])
    own[low, :] = dot_nn(gg[low, :], gate_o[0]) + dot_nn(ug[low, :], up_o[0])
    own[high, :] = dot_nn(gg[high, :], gate_o[1]) + dot_nn(ug[high, :], up_o[1])


def weight_kernel(head, *refs):
    blocks = refs[0:8]
    sides = len(refs[8:]) // 2
    lefts, results = refs[8 : 8 + sides], refs[8 + sides :]
    width = blocks[0].shape[1]
    offsets = (0, 3, 1, 2)
    for q in range(4):
        col = pl.multiple_of(((head[0] + offsets[q]) % 4) * width, width)
        for e in range(LOCAL):
            rows = blocks[e].shape[0]
            data = blocks[2 * q + e][...]
            for left, result in zip(lefts, results):
                part = dot_tn(left[pl.ds(e * rows, rows), :], data)
                result[e, :, pl.ds(col, width)] = part.astype(BF)


def round_ring(low, high):
    right_low = turned(low, 1)
    left_high = turned(high, -1)
    right_high = turned(high, 1)
    left_low = turned(low, -1)
    far_low = turned(right_low, 1)
    far_high = turned(left_high, -1)
    return [low, high, right_low, right_high, left_low, left_high, far_low, far_high]


def join_kernel(head, *refs):
    parts, result = refs[:4], refs[4]
    width = parts[0].shape[1]
    for part, offset in zip(parts, (0, 3, 1, 2)):
        col = pl.multiple_of(((head[0] + offset) % 4) * width, width)
        result[:, pl.ds(col, width)] = part[...]


def exchange(send, count):
    half = send.shape[1]
    return lax.all_to_all(
        send.reshape(count, GROUP, half), "ctx", split_axis=0, concat_axis=0, tiled=True
    ).reshape(count * GROUP, half)


def dispatch(send, head, count, lanes):
    half = send.shape[1]
    recv = exchange(send, count)
    low, high = call(
        untangle_kernel,
        head,
        [full(recv)],
        [out((count * CAP, 2 * half), BF), out((count * CAP, 2 * half), BF)],
        [[pltpu.VMEM((count * GROUP, lanes), F32) for _ in range(half // lanes)]],
    )
    return round_ring(low, high)


def attention(query_rows, window_kv, attn_out, grad_attn, segment_ids, kv_width):
    att_rows = query_rows.shape[0]
    kv_local = kv_width // HD
    group_size = HQ // KVH
    window = (REACH + 1) * att_rows
    score_scale = HD ** (-0.5)
    ctx_index = lax.axis_index("ctx")
    window_key = window_kv[:, :kv_width].reshape(window, kv_local, HD)
    window_value = window_kv[:, kv_width:].reshape(window, kv_local, HD)
    query_pos = ctx_index * att_rows + jnp.arange(att_rows, dtype=jnp.int32)
    key_pos = (ctx_index - REACH) * att_rows + jnp.arange(window, dtype=jnp.int32)
    padded_segment = jnp.concatenate([jnp.full((REACH * att_rows,), -1, jnp.int32), segment_ids])
    key_seg = lax.dynamic_slice_in_dim(padded_segment, ctx_index * att_rows, window, 0)
    query_seg = lax.dynamic_slice_in_dim(segment_ids, ctx_index * att_rows, att_rows, 0)
    visible = (key_pos[None, :] <= query_pos[:, None]) & (key_seg[None, :] == query_seg[:, None])
    query_heads = query_rows.reshape(att_rows, kv_local, group_size, HD)
    out_heads = attn_out.reshape(att_rows, kv_local, group_size, HD)
    grad_heads = grad_attn.reshape(att_rows, kv_local, group_size, HD)
    scores = (
        jnp.einsum("ajgd,tjd->jgat", query_heads, window_key, preferred_element_type=F32)
        * score_scale
    )
    row_peak = jnp.max(jnp.where(visible, scores, -jnp.inf), axis=-1, keepdims=True)
    weights_exp = jnp.exp(jnp.where(visible, scores - row_peak, -jnp.inf))
    probs = weights_exp / jnp.sum(weights_exp, axis=-1, keepdims=True)
    row_delta = jnp.einsum("ajgd,ajgd->jga", grad_heads, out_heads, preferred_element_type=F32)
    prob_grad = jnp.einsum("ajgd,tjd->jgat", grad_heads, window_value, preferred_element_type=F32)
    score_grad = (probs * (prob_grad - row_delta[..., None])).astype(BF)
    probs_low = probs.astype(BF)
    grad_query = (
        (score_scale * jnp.einsum("jgat,tjd->ajgd", score_grad, window_key, preferred_element_type=F32))
        .astype(BF)
        .reshape(att_rows, -1)
    )
    key_terms = (
        score_scale
        * jnp.einsum("jgat,ajgd->tjd", score_grad, query_heads, preferred_element_type=F32)
    ).reshape(window, kv_width)
    value_terms = jnp.einsum(
        "jgat,ajgd->tjd", probs_low, grad_heads, preferred_element_type=F32
    ).reshape(window, kv_width)
    return grad_query, jnp.concatenate([key_terms, value_terms], axis=1)


def body(
    tokens,
    grad_out,
    expert_ids,
    gate_probs,
    w_gate,
    w_up,
    w_down,
    query_rows,
    key_rows,
    value_rows,
    attn_out,
    grad_attn,
    segment_ids,
):
    tok_count, width = tokens.shape
    count = lax.axis_size("ctx")
    quarter = width // 4
    half = quarter // 2
    lanes = min(half, 128)
    hidden_local = w_gate.shape[1]
    head = lax.axis_index("head").astype(jnp.int32).reshape(1)
    experts = count * LOCAL
    slots = count * GROUP
    rows = count * CAP
    kv_width = key_rows.shape[1]
    att_rows = query_rows.shape[0]

    kv = jnp.concatenate([key_rows, value_rows], axis=1)
    kv_blocks = [passed_along(kv, "ctx", distance) for distance in range(REACH, 0, -1)]

    send_rows, pick, scaled = call(
        route_kernel,
        head,
        [
            full(expert_ids.T),
            full(gate_probs.T),
            full(pattern_table(tok_count)),
            (tokens, column_block(tokens.shape, 0)),
        ],
        [out((slots, half), BF), out((slots, 2 * tok_count), BF), out((slots, 2 * tok_count), BF)],
        [pltpu.VMEM((experts, tok_count), F32), pltpu.VMEM((experts, tok_count), F32)],
    )
    (send_grads,) = call(
        select_kernel,
        head,
        [full(scaled), (grad_out, column_block(grad_out.shape, 0))],
        [out((slots, half), BF)],
    )
    row_blocks = dispatch(send_rows, head, count, lanes)
    grad_blocks = dispatch(send_grads, head, count, lanes)

    gate_at = lambda offset: (w_gate, column_block(w_gate.shape, offset))
    up_at = lambda offset: (w_up, column_block(w_up.shape, offset))
    down_at = lambda offset: (w_down, column_block(w_down.shape, offset))
    order = (0, 3, 1, 2)
    act, slope, hidden = call(
        pre_kernel,
        head,
        [full(b) for b in row_blocks] + [gate_at(o) for o in order] + [up_at(o) for o in order],
        [
            out((2 * rows, hidden_local), F32),
            out((2 * rows, hidden_local), F32),
            out((2 * rows, hidden_local), BF),
        ],
    )
    (got_near,) = call(
        near_kernel,
        head,
        [full(b) for b in grad_blocks[:6]] + [down_at(o) for o in order[:3]],
        [out((2 * rows, hidden_local), F32)],
    )
    gg, ug, far_low, far_high = call(
        grad_kernel,
        head,
        [full(b) for b in grad_blocks[6:]]
        + [down_at(2), full(got_near), full(act), full(slope), gate_at(2), up_at(2)],
        [
            out((2 * rows, hidden_local), BF),
            out((2 * rows, hidden_local), BF),
            out((rows, quarter), BF),
            out((rows, quarter), BF),
        ],
    )
    near_low = turned(far_low, 1)
    near_high = turned(far_high, -1)
    p0, p1, m0, m1, own = call(
        back_kernel,
        head,
        [full(gg), full(ug), gate_at(1), up_at(1), gate_at(3), up_at(3), gate_at(0), up_at(0)],
        [
            out((rows, quarter), F32),
            out((rows, quarter), BF),
            out((rows, quarter), BF),
            out((rows, quarter), F32),
            out((2 * rows, quarter), F32),
        ],
    )
    left_a = turned(p1, 1)
    right_a = turned(m0, -1)
    left_b = turned((p0 + near_low.astype(F32)).astype(BF), 1)
    right_b = turned((m1 + near_high.astype(F32)).astype(BF), -1)
    (send_back,) = call(
        tangle_kernel,
        head,
        [full(own), full(left_a), full(left_b), full(right_a), full(right_b)],
        [out((slots, half), BF)],
        [[pltpu.VMEM((slots, lanes), F32) for _ in range(half // lanes)]],
    )
    returned = exchange(send_back, count)
    summed = dot_tn(pick, returned)
    token_part = jnp.concatenate([summed[:tok_count], summed[tok_count:]], axis=1).astype(BF)
    parts = [token_part] + [turned(token_part, distance) for distance in (1, 3, 2)]
    (grad_tokens,) = call(join_kernel, head, [full(p) for p in parts], [out(tokens.shape, BF)])

    weight_out = out(w_gate.shape, BF)
    grad_gate, grad_up = call(
        weight_kernel,
        head,
        [full(b) for b in row_blocks] + [full(gg), full(ug)],
        [weight_out, weight_out],
    )
    (grad_down,) = call(
        weight_kernel, head, [full(b) for b in grad_blocks] + [full(hidden)], [weight_out]
    )

    grad_query, terms = attention(
        query_rows,
        jnp.concatenate(kv_blocks + [kv], axis=0),
        attn_out,
        grad_attn,
        segment_ids,
        kv_width,
    )
    total = terms[REACH * att_rows :]
    for distance in range(1, REACH + 1):
        offset = (REACH - distance) * att_rows
        total = total + passed_along(terms[offset : offset + att_rows], "ctx", -distance)
    total = total.astype(BF)
    return (
        grad_tokens,
        grad_gate,
        grad_up,
        grad_down,
        grad_query,
        total[:, :kv_width],
        total[:, kv_width:],
    )


def solution(mesh):
    placed = (
        P("ctx", None),
        P("ctx", None),
        P("ctx", None),
        P("ctx", None),
        P("ctx", "head", None),
        P("ctx", "head", None),
        P("ctx", "head", None),
        P("ctx", "head"),
        P("ctx", "head"),
        P("ctx", "head"),
        P("ctx", "head"),
        P("ctx", "head"),
        P(),
    )
    return jax.shard_map(
        body,
        mesh=mesh,
        in_specs=placed,
        out_specs=(
            P("ctx", None),
            P("ctx", "head", None),
            P("ctx", "head", None),
            P("ctx", "head", None),
            P("ctx", "head"),
            P("ctx", "head"),
            P("ctx", "head"),
        ),
        check_vma=False,
    )
```

```python
import jax
import jax.numpy as jnp
from jax import lax
from jax.experimental import pallas as pl
from jax.experimental.pallas import tpu as pltpu
from jax.sharding import PartitionSpec as P


HD = 128
REACH = 3
CAP = 10
LOCAL = 2
SLOTS = LOCAL * CAP
GROUP = 2 * SLOTS
BF = jnp.bfloat16
F32 = jnp.float32


def passed_along(block, axis, distance):
    devices = range(lax.axis_size(axis))
    route = [(i - distance, i) for i in devices if i - distance in devices]
    return lax.ppermute(block, axis, route)


def turned(block, distance):
    count = lax.axis_size("head")
    return lax.ppermute(block, "head", [(i, (i + distance) % count) for i in range(count)])


def dot_nt(a, b):
    return lax.dot_general(a, b, (((1,), (1,)), ((), ())), preferred_element_type=F32)


def dot_nn(a, b):
    return lax.dot_general(a, b, (((1,), (0,)), ((), ())), preferred_element_type=F32)


def dot_tn(a, b):
    return lax.dot_general(a, b, (((0,), (0,)), ((), ())), preferred_element_type=F32)


def column_block(shape, offset):
    block = shape[:-1] + (shape[-1] // 4,)
    lead = (0,) * (len(shape) - 1)
    return pl.BlockSpec(block, lambda i, head, lead=lead, offset=offset: lead + ((head[0] + offset) % 4,))


def whole(shape):
    zeros = (0,) * len(shape)
    return pl.BlockSpec(shape, lambda i, head, zeros=zeros: zeros)


def call(kernel, head, ins, outs, scratch=()):
    return launched(kernel, head, ins, outs, scratch)


def launched(kernel, head, ins, outs, scratch):
    arrays = [a for a, _ in ins]
    return pl.pallas_call(
        kernel,
        grid_spec=pltpu.PrefetchScalarGridSpec(
            num_scalar_prefetch=1,
            grid=(1,),
            in_specs=[s for _, s in ins],
            out_specs=[s for _, s in outs],
            scratch_shapes=list(scratch),
        ),
        out_shape=[o for o, _ in outs],
        compiler_params=pltpu.CompilerParams(vmem_limit_bytes=56 << 20),
    )(head, *arrays)


def full(a):
    return (a, whole(a.shape))


def out(shape, dtype):
    return (jax.ShapeDtypeStruct(shape, dtype), whole(shape))


def route_kernel(head, ids, probs, tok, rows_ref, pick_ref, scaled_ref, rank_s, prob_s):
    experts, count = rank_s.shape
    where_e = lax.broadcasted_iota(jnp.int32, (experts, count), 0)
    hits = jnp.zeros((experts, count), F32)
    chance = jnp.zeros((experts, count), F32)
    weights = probs[...].astype(F32)
    for k in range(ids.shape[0]):
        hit = ids[k : k + 1, :] == where_e
        hits = jnp.where(hit, 1.0, hits)
        chance = jnp.where(hit, weights[k : k + 1, :], chance)
    first = lax.broadcasted_iota(jnp.int32, (count, count), 0)
    second = lax.broadcasted_iota(jnp.int32, (count, count), 1)
    before = jnp.where(first < second, 1.0, 0.0).astype(BF)
    rank = dot_nn(hits.astype(BF), before)
    rank_s[...] = jnp.where(hits > 0.0, rank, -1.0)
    prob_s[...] = chance
    row = lax.broadcasted_iota(jnp.int32, (2 * GROUP, count), 0)
    run = jnp.zeros_like(row)
    for k in range(1, 2 * GROUP // CAP):
        run = run + jnp.where(row >= k * CAP, 1, 0)
    place = (row - CAP * run).astype(F32)
    which = jnp.where(run >= 2 * LOCAL, LOCAL, 0) + (run & 1)
    in_low = (run & LOCAL) == 0

    def step(i, carry):
        base = i * (2 * LOCAL)
        value = rank_s[pl.ds(base, 1), :]
        weight = prob_s[pl.ds(base, 1), :]
        for j in range(1, 2 * LOCAL):
            mine = which == j
            value = jnp.where(mine, rank_s[pl.ds(base + j, 1), :], value)
            weight = jnp.where(mine, prob_s[pl.ds(base + j, 1), :], weight)
        match = jnp.where(value == place, 1.0, 0.0)
        weight = match * weight
        at = pl.multiple_of(i * 2 * GROUP, 2 * GROUP)
        zero = jnp.zeros_like(match)
        pick_ref[pl.ds(at, 2 * GROUP), 0:count] = jnp.where(in_low, match, zero).astype(BF)
        pick_ref[pl.ds(at, 2 * GROUP), count : 2 * count] = jnp.where(in_low, zero, match).astype(BF)
        scaled_ref[pl.ds(at, 2 * GROUP), 0:count] = jnp.where(in_low, weight, zero).astype(BF)
        scaled_ref[pl.ds(at, 2 * GROUP), count : 2 * count] = jnp.where(in_low, zero, weight).astype(BF)
        return carry

    lax.fori_loop(0, experts // (2 * LOCAL), step, 0)
    half = tok.shape[1] // 2
    stacked = jnp.concatenate([tok[:, :half], tok[:, half:]], axis=0)
    rows_ref[...] = dot_nn(pick_ref[...], stacked).astype(BF)


def select_kernel(head, scaled, own, far, own_ref, far_ref):
    for tok, ref in ((own, own_ref), (far, far_ref)):
        half = tok.shape[1] // 2
        stacked = jnp.concatenate([tok[:, :half], tok[:, half:]], axis=0)
        ref[...] = dot_nn(scaled[...], stacked).astype(BF)


def untangle_kernel(head, recv, low_ref, high_ref, wide):
    sources = recv.shape[0] // GROUP
    half = recv.shape[1]
    lanes = wide[0].shape[1]
    for p in range(half // lanes):
        wide[p][...] = recv[:, p * lanes : (p + 1) * lanes].astype(F32)
    for e, ref in ((0, low_ref), (1, high_ref)):
        for c in range(CAP):
            for part in range(2):
                for p in range(half // lanes):
                    rows = wide[p][pl.ds(part * SLOTS + e * CAP + c, sources, stride=GROUP), :]
                    col = part * half + p * lanes
                    ref[c * sources : (c + 1) * sources, col : col + lanes] = rows.astype(BF)


def tangle_kernel(head, own, left_a, left_b, right_a, right_b, send_ref, wide):
    rows = own.shape[0] // 2
    sources = rows // CAP
    half = own.shape[1] // 2
    lanes = wide[0].shape[1]
    for e, (a, b) in ((0, (left_b, right_a)), (1, (left_a, right_b))):
        for c in range(CAP):
            for part in range(2):
                for p in range(half // lanes):
                    col = part * half + p * lanes
                    at = c * sources
                    total = (
                        own[e * rows + at : e * rows + at + sources, col : col + lanes]
                        + a[at : at + sources, col : col + lanes].astype(F32)
                        + b[at : at + sources, col : col + lanes].astype(F32)
                    )
                    wide[p][pl.ds(part * SLOTS + e * CAP + c, sources, stride=GROUP), :] = total
    for p in range(half // lanes):
        send_ref[:, p * lanes : (p + 1) * lanes] = wide[p][...].astype(BF)


def pre_kernel(head, *refs):
    blocks, gates, ups = refs[0:8], refs[8:12], refs[12:16]
    act_ref, slope_ref, hidden_ref = refs[16:]
    for e in range(LOCAL):
        rows = blocks[e].shape[0]
        gate = dot_nt(blocks[e][...], gates[0][e])
        up = dot_nt(blocks[e][...], ups[0][e])
        for q in range(1, 4):
            gate = gate + dot_nt(blocks[2 * q + e][...], gates[q][e])
            up = up + dot_nt(blocks[2 * q + e][...], ups[q][e])
        sig = jax.nn.sigmoid(gate)
        active = gate * sig
        at = pl.ds(e * rows, rows)
        act_ref[at, :] = active
        slope_ref[at, :] = up * sig * (1.0 + gate * (1.0 - sig))
        hidden_ref[at, :] = (active * up).astype(BF)


def near_kernel(head, *refs):
    blocks, downs, got_ref = refs[0:6], refs[6:9], refs[9]
    for e in range(LOCAL):
        rows = blocks[e].shape[0]
        got = dot_nt(blocks[e][...], downs[0][e])
        for q in range(1, 3):
            got = got + dot_nt(blocks[2 * q + e][...], downs[q][e])
        got_ref[pl.ds(e * rows, rows), :] = got


def grad_kernel(head, low, high, down, got_near, act, slope, gate_far, up_far, *outs):
    gg_ref, ug_ref, far_low, far_high = outs
    for e, block, far in ((0, low, far_low), (1, high, far_high)):
        rows = block.shape[0]
        at = pl.ds(e * rows, rows)
        got = got_near[at, :] + dot_nt(block[...], down[e])
        gg = (got * slope[at, :]).astype(BF)
        ug = (got * act[at, :]).astype(BF)
        gg_ref[at, :] = gg
        ug_ref[at, :] = ug
        far[...] = (dot_nn(gg, gate_far[e]) + dot_nn(ug, up_far[e])).astype(BF)


def back_kernel(head, gg, ug, gate_p, up_p, gate_m, up_m, gate_o, up_o, p0, p1, m0, m1, own):
    rows = gg.shape[0] // 2
    low, high = pl.ds(0, rows), pl.ds(rows, rows)
    p1[...] = (dot_nn(gg[high, :], gate_p[1]) + dot_nn(ug[high, :], up_p[1])).astype(BF)
    m0[...] = (dot_nn(gg[low, :], gate_m[0]) + dot_nn(ug[low, :], up_m[0])).astype(BF)
    p0[...] = dot_nn(gg[low, :], gate_p[0]) + dot_nn(ug[low, :], up_p[0])
    m1[...] = dot_nn(gg[high, :], gate_m[1]) + dot_nn(ug[high, :], up_m[1])
    own[low, :] = dot_nn(gg[low, :], gate_o[0]) + dot_nn(ug[low, :], up_o[0])
    own[high, :] = dot_nn(gg[high, :], gate_o[1]) + dot_nn(ug[high, :], up_o[1])


def weight_kernel(head, *refs):
    blocks = refs[0:8]
    sides = len(refs[8:]) // 2
    lefts, results = refs[8 : 8 + sides], refs[8 + sides :]
    width = blocks[0].shape[1]
    offsets = (0, 3, 1, 2)
    for q in range(4):
        col = pl.multiple_of(((head[0] + offsets[q]) % 4) * width, width)
        for e in range(LOCAL):
            rows = blocks[e].shape[0]
            data = blocks[2 * q + e][...]
            for left, result in zip(lefts, results):
                part = dot_tn(left[pl.ds(e * rows, rows), :], data)
                result[e, :, pl.ds(col, width)] = part.astype(BF)


def near_ring(low, high):
    right_low = turned(low, 1)
    left_high = turned(high, -1)
    right_high = turned(high, 1)
    left_low = turned(low, -1)
    return [low, high, right_low, right_high, left_low, left_high]


def join_kernel(head, *refs):
    parts, result = refs[:4], refs[4]
    width = parts[0].shape[1]
    for part, offset in zip(parts, (0, 3, 1, 2)):
        col = pl.multiple_of(((head[0] + offset) % 4) * width, width)
        result[:, pl.ds(col, width)] = part[...]


def exchange(send, count):
    half = send.shape[1]
    return lax.all_to_all(
        send.reshape(count, GROUP, half), "ctx", split_axis=0, concat_axis=0, tiled=True
    ).reshape(count * GROUP, half)


def dispatch(send, head, count, lanes):
    half = send.shape[1]
    recv = exchange(send, count)
    low, high = call(
        untangle_kernel,
        head,
        [full(recv)],
        [out((count * CAP, 2 * half), BF), out((count * CAP, 2 * half), BF)],
        [[pltpu.VMEM((count * GROUP, lanes), F32) for _ in range(half // lanes)]],
    )
    return low, high


def attention_kernel(head, query, out_ref, grad, kv3, kv2, kv1, kv0, query_seg, key_seg, *refs):
    grad_query, t3, t2, t1, t0, window, key_sum, value_sum = refs
    rows = query.shape[0]
    span = window.shape[0]
    scale = HD ** (-0.5)
    for at, block in enumerate((kv3, kv2, kv1, kv0)):
        window[at * rows : (at + 1) * rows, :] = block[...]
    key_sum[...] = jnp.zeros_like(key_sum)
    value_sum[...] = jnp.zeros_like(value_sum)
    query_at = lax.broadcasted_iota(jnp.int32, (rows, span), 0) + (span - rows)
    key_at = lax.broadcasted_iota(jnp.int32, (rows, span), 1)
    visible = (key_at <= query_at) & (query_seg[...] == key_seg[...])

    def one_head(g, carry):
        lanes = pl.ds(pl.multiple_of(g * HD, HD), HD)
        keys, values = window[:, :HD], window[:, HD:]
        q, dout = query[:, lanes], grad[:, lanes]
        scores = dot_nt(q, keys) * scale
        peak = jnp.max(jnp.where(visible, scores, -jnp.inf), axis=1, keepdims=True)
        weights = jnp.exp(jnp.where(visible, scores - peak, -jnp.inf))
        probs = weights / jnp.sum(weights, axis=1, keepdims=True)
        delta = jnp.sum(dout.astype(F32) * out_ref[:, lanes].astype(F32), axis=1, keepdims=True)
        score_grad = (probs * (dot_nt(dout, values) - delta)).astype(BF)
        grad_query[:, lanes] = (scale * dot_nn(score_grad, keys)).astype(BF)
        key_sum[...] += dot_tn(score_grad, q)
        value_sum[...] += dot_tn(probs.astype(BF), dout)
        return carry

    lax.fori_loop(0, query.shape[1] // HD, one_head, 0)
    for at, ref in enumerate((t3, t2, t1, t0)):
        part = pl.ds(at * rows, rows)
        ref[:, :HD] = scale * key_sum[part, :]
        ref[:, HD:] = value_sum[part, :]


def attention(head, query_rows, kv_blocks, attn_out, grad_attn, segment_ids):
    rows = query_rows.shape[0]
    window = (REACH + 1) * rows
    at = lax.axis_index("ctx") * rows
    padded = jnp.concatenate([jnp.full((REACH * rows,), -1, jnp.int32), segment_ids])
    key_seg = lax.dynamic_slice_in_dim(padded, at, window, 0).reshape(1, window)
    query_seg = lax.dynamic_slice_in_dim(segment_ids, at, rows, 0).reshape(rows, 1)
    return call(
        attention_kernel,
        head,
        [full(query_rows), full(attn_out), full(grad_attn)]
        + [full(b) for b in kv_blocks]
        + [full(query_seg), full(key_seg)],
        [out(query_rows.shape, BF)] + [out((rows, 2 * HD), F32) for _ in range(REACH + 1)],
        [
            pltpu.VMEM((window, 2 * HD), BF),
            pltpu.VMEM((window, HD), F32),
            pltpu.VMEM((window, HD), F32),
        ],
    )


def body(
    tokens,
    grad_out,
    expert_ids,
    gate_probs,
    w_gate,
    w_up,
    w_down,
    query_rows,
    key_rows,
    value_rows,
    attn_out,
    grad_attn,
    segment_ids,
):
    tok_count, width = tokens.shape
    count = lax.axis_size("ctx")
    quarter = width // 4
    half = quarter // 2
    lanes = min(half, 128)
    hidden_local = w_gate.shape[1]
    head = lax.axis_index("head").astype(jnp.int32).reshape(1)
    experts = count * LOCAL
    slots = count * GROUP
    rows = count * CAP
    kv_width = key_rows.shape[1]

    kv = jnp.concatenate([key_rows, value_rows], axis=1)
    kv_blocks = [passed_along(kv, "ctx", distance) for distance in range(REACH, 0, -1)]

    send_rows, pick, scaled = call(
        route_kernel,
        head,
        [
            full(expert_ids.T),
            full(gate_probs.T),
            (tokens, column_block(tokens.shape, 0)),
        ],
        [out((slots, half), BF), out((slots, 2 * tok_count), BF), out((slots, 2 * tok_count), BF)],
        [pltpu.VMEM((experts, tok_count), F32), pltpu.VMEM((experts, tok_count), F32)],
    )
    send_grads, send_far = call(
        select_kernel,
        head,
        [
            full(scaled),
            (grad_out, column_block(grad_out.shape, 0)),
            (grad_out, column_block(grad_out.shape, 2)),
        ],
        [out((slots, half), BF), out((slots, half), BF)],
    )
    row_blocks = near_ring(*dispatch(send_rows, head, count, lanes))
    row_blocks += [turned(row_blocks[2], 1), turned(row_blocks[5], -1)]
    grad_blocks = near_ring(*dispatch(send_grads, head, count, lanes))
    grad_blocks += dispatch(send_far, head, count, lanes)

    gate_at = lambda offset: (w_gate, column_block(w_gate.shape, offset))
    up_at = lambda offset: (w_up, column_block(w_up.shape, offset))
    down_at = lambda offset: (w_down, column_block(w_down.shape, offset))
    order = (0, 3, 1, 2)
    act, slope, hidden = call(
        pre_kernel,
        head,
        [full(b) for b in row_blocks] + [gate_at(o) for o in order] + [up_at(o) for o in order],
        [
            out((2 * rows, hidden_local), F32),
            out((2 * rows, hidden_local), F32),
            out((2 * rows, hidden_local), BF),
        ],
    )
    (got_near,) = call(
        near_kernel,
        head,
        [full(b) for b in grad_blocks[:6]] + [down_at(o) for o in order[:3]],
        [out((2 * rows, hidden_local), F32)],
    )
    gg, ug, far_low, far_high = call(
        grad_kernel,
        head,
        [full(b) for b in grad_blocks[6:]]
        + [down_at(2), full(got_near), full(act), full(slope), gate_at(2), up_at(2)],
        [
            out((2 * rows, hidden_local), BF),
            out((2 * rows, hidden_local), BF),
            out((rows, quarter), BF),
            out((rows, quarter), BF),
        ],
    )
    near_low = turned(far_low, 1)
    near_high = turned(far_high, -1)
    p0, p1, m0, m1, own = call(
        back_kernel,
        head,
        [full(gg), full(ug), gate_at(1), up_at(1), gate_at(3), up_at(3), gate_at(0), up_at(0)],
        [
            out((rows, quarter), F32),
            out((rows, quarter), BF),
            out((rows, quarter), BF),
            out((rows, quarter), F32),
            out((2 * rows, quarter), F32),
        ],
    )
    left_a = turned(p1, 1)
    right_a = turned(m0, -1)
    left_b = turned((p0 + near_low.astype(F32)).astype(BF), 1)
    right_b = turned((m1 + near_high.astype(F32)).astype(BF), -1)
    (send_back,) = call(
        tangle_kernel,
        head,
        [full(own), full(left_a), full(left_b), full(right_a), full(right_b)],
        [out((slots, half), BF)],
        [[pltpu.VMEM((slots, lanes), F32) for _ in range(half // lanes)]],
    )
    returned = exchange(send_back, count)
    summed = dot_tn(pick, returned)
    token_part = jnp.concatenate([summed[:tok_count], summed[tok_count:]], axis=1).astype(BF)
    parts = [token_part] + [turned(token_part, distance) for distance in (1, 3, 2)]
    (grad_tokens,) = call(join_kernel, head, [full(p) for p in parts], [out(tokens.shape, BF)])

    weight_out = out(w_gate.shape, BF)
    grad_gate, grad_up = call(
        weight_kernel,
        head,
        [full(b) for b in row_blocks] + [full(gg), full(ug)],
        [weight_out, weight_out],
    )
    (grad_down,) = call(
        weight_kernel, head, [full(b) for b in grad_blocks] + [full(hidden)], [weight_out]
    )

    grad_query, *terms = attention(
        head, query_rows, kv_blocks + [kv], attn_out, grad_attn, segment_ids
    )
    total = terms[REACH]
    for distance in range(1, REACH + 1):
        total = total + passed_along(terms[REACH - distance], "ctx", -distance)
    total = total.astype(BF)
    return (
        grad_tokens,
        grad_gate,
        grad_up,
        grad_down,
        grad_query,
        total[:, :kv_width],
        total[:, kv_width:],
    )


def solution(mesh):
    placed = (
        P("ctx", None),
        P("ctx", None),
        P("ctx", None),
        P("ctx", None),
        P("ctx", "head", None),
        P("ctx", "head", None),
        P("ctx", "head", None),
        P("ctx", "head"),
        P("ctx", "head"),
        P("ctx", "head"),
        P("ctx", "head"),
        P("ctx", "head"),
        P(),
    )
    return jax.shard_map(
        body,
        mesh=mesh,
        in_specs=placed,
        out_specs=(
            P("ctx", None),
            P("ctx", "head", None),
            P("ctx", "head", None),
            P("ctx", "head", None),
            P("ctx", "head"),
            P("ctx", "head"),
            P("ctx", "head"),
        ),
        check_vma=False,
    )
```

```python
import jax
import jax.numpy as jnp
from jax import lax
from jax.experimental import pallas as pl
from jax.experimental.pallas import tpu as pltpu
from jax.sharding import PartitionSpec as P


HD = 128
REACH = 3
CAP = 10
LOCAL = 2
SLOTS = LOCAL * CAP
GROUP = 2 * SLOTS
BF = jnp.bfloat16
F32 = jnp.float32


def passed_along(block, axis, distance):
    devices = range(lax.axis_size(axis))
    route = [(i - distance, i) for i in devices if i - distance in devices]
    return lax.ppermute(block, axis, route)


def turned(block, distance):
    count = lax.axis_size("head")
    return lax.ppermute(block, "head", [(i, (i + distance) % count) for i in range(count)])


def dot_nt(a, b):
    return lax.dot_general(a, b, (((1,), (1,)), ((), ())), preferred_element_type=F32)


def dot_nn(a, b):
    return lax.dot_general(a, b, (((1,), (0,)), ((), ())), preferred_element_type=F32)


def dot_tn(a, b):
    return lax.dot_general(a, b, (((0,), (0,)), ((), ())), preferred_element_type=F32)


def column_block(shape, offset):
    block = shape[:-1] + (shape[-1] // 4,)
    lead = (0,) * (len(shape) - 1)
    return pl.BlockSpec(block, lambda i, head, lead=lead, offset=offset: lead + ((head[0] + offset) % 4,))


def whole(shape):
    zeros = (0,) * len(shape)
    return pl.BlockSpec(shape, lambda i, head, zeros=zeros: zeros)


def call(kernel, head, ins, outs, scratch=()):
    return launched(kernel, head, ins, outs, scratch)


def launched(kernel, head, ins, outs, scratch):
    arrays = [a for a, _ in ins]
    return pl.pallas_call(
        kernel,
        grid_spec=pltpu.PrefetchScalarGridSpec(
            num_scalar_prefetch=1,
            grid=(1,),
            in_specs=[s for _, s in ins],
            out_specs=[s for _, s in outs],
            scratch_shapes=list(scratch),
        ),
        out_shape=[o for o, _ in outs],
        compiler_params=pltpu.CompilerParams(vmem_limit_bytes=56 << 20),
    )(head, *arrays)


def full(a):
    return (a, whole(a.shape))


def out(shape, dtype):
    return (jax.ShapeDtypeStruct(shape, dtype), whole(shape))


def route_kernel(head, ids, probs, tok, rows_ref, pick_ref, scaled_ref, rank_s, prob_s):
    experts, count = rank_s.shape
    where_e = lax.broadcasted_iota(jnp.int32, (experts, count), 0)
    hits = jnp.zeros((experts, count), F32)
    chance = jnp.zeros((experts, count), F32)
    weights = probs[...].astype(F32)
    for k in range(ids.shape[0]):
        hit = ids[k : k + 1, :] == where_e
        hits = jnp.where(hit, 1.0, hits)
        chance = jnp.where(hit, weights[k : k + 1, :], chance)
    first = lax.broadcasted_iota(jnp.int32, (count, count), 0)
    second = lax.broadcasted_iota(jnp.int32, (count, count), 1)
    before = jnp.where(first < second, 1.0, 0.0).astype(BF)
    rank = dot_nn(hits.astype(BF), before)
    rank_s[...] = jnp.where(hits > 0.0, rank, -1.0)
    prob_s[...] = chance
    row = lax.broadcasted_iota(jnp.int32, (2 * GROUP, count), 0)
    run = jnp.zeros_like(row)
    for k in range(1, 2 * GROUP // CAP):
        run = run + jnp.where(row >= k * CAP, 1, 0)
    place = (row - CAP * run).astype(F32)
    which = jnp.where(run >= 2 * LOCAL, LOCAL, 0) + (run & 1)
    in_low = (run & LOCAL) == 0

    def step(i, carry):
        base = i * (2 * LOCAL)
        value = rank_s[pl.ds(base, 1), :]
        weight = prob_s[pl.ds(base, 1), :]
        for j in range(1, 2 * LOCAL):
            mine = which == j
            value = jnp.where(mine, rank_s[pl.ds(base + j, 1), :], value)
            weight = jnp.where(mine, prob_s[pl.ds(base + j, 1), :], weight)
        match = jnp.where(value == place, 1.0, 0.0)
        weight = match * weight
        at = pl.multiple_of(i * 2 * GROUP, 2 * GROUP)
        zero = jnp.zeros_like(match)
        pick_ref[pl.ds(at, 2 * GROUP), 0:count] = jnp.where(in_low, match, zero).astype(BF)
        pick_ref[pl.ds(at, 2 * GROUP), count : 2 * count] = jnp.where(in_low, zero, match).astype(BF)
        scaled_ref[pl.ds(at, 2 * GROUP), 0:count] = jnp.where(in_low, weight, zero).astype(BF)
        scaled_ref[pl.ds(at, 2 * GROUP), count : 2 * count] = jnp.where(in_low, zero, weight).astype(BF)
        return carry

    lax.fori_loop(0, experts // (2 * LOCAL), step, 0)
    half = tok.shape[1] // 2
    stacked = jnp.concatenate([tok[:, :half], tok[:, half:]], axis=0)
    rows_ref[...] = dot_nn(pick_ref[...], stacked).astype(BF)


def select_kernel(head, scaled, tok, rows_ref):
    half = tok.shape[1] // 2
    stacked = jnp.concatenate([tok[:, :half], tok[:, half:]], axis=0)
    rows_ref[...] = dot_nn(scaled[...], stacked).astype(BF)


def untangle_kernel(head, recv, low_ref, high_ref, wide):
    sources = recv.shape[0] // GROUP
    half = recv.shape[1]
    lanes = wide[0].shape[1]
    for p in range(half // lanes):
        wide[p][...] = recv[:, p * lanes : (p + 1) * lanes].astype(F32)
    for e, ref in ((0, low_ref), (1, high_ref)):
        for c in range(CAP):
            for part in range(2):
                for p in range(half // lanes):
                    rows = wide[p][pl.ds(part * SLOTS + e * CAP + c, sources, stride=GROUP), :]
                    col = part * half + p * lanes
                    ref[c * sources : (c + 1) * sources, col : col + lanes] = rows.astype(BF)


def pre_kernel(head, *refs):
    blocks, gates, ups = refs[0:8], refs[8:12], refs[12:16]
    act_ref, slope_ref, *hidden_refs = refs[16:]
    for e in range(LOCAL):
        rows = blocks[e].shape[0]
        gate = dot_nt(blocks[e][...], gates[0][e])
        up = dot_nt(blocks[e][...], ups[0][e])
        for q in range(1, 4):
            gate = gate + dot_nt(blocks[2 * q + e][...], gates[q][e])
            up = up + dot_nt(blocks[2 * q + e][...], ups[q][e])
        sig = jax.nn.sigmoid(gate)
        active = gate * sig
        at = pl.ds(e * rows, rows)
        act_ref[at, :] = active
        slope_ref[at, :] = up * sig * (1.0 + gate * (1.0 - sig))
        hidden_refs[e][...] = (active * up).astype(BF)


def near_kernel(head, *refs):
    blocks, downs, got_ref = refs[0:6], refs[6:9], refs[9]
    for e in range(LOCAL):
        rows = blocks[e].shape[0]
        got = dot_nt(blocks[e][...], downs[0][e])
        for q in range(1, 3):
            got = got + dot_nt(blocks[2 * q + e][...], downs[q][e])
        got_ref[pl.ds(e * rows, rows), :] = got


def grad_kernel(head, low, high, down, got_near, act, slope, gu_low, gu_high):
    units = act.shape[1]
    for e, block, ref in ((0, low, gu_low), (1, high, gu_high)):
        rows = block.shape[0]
        at = pl.ds(e * rows, rows)
        got = got_near[at, :] + dot_nt(block[...], down[e])
        ref[:, :units] = (got * slope[at, :]).astype(BF)
        ref[:, units:] = (got * act[at, :]).astype(BF)


def columns_kernel(head, *refs):
    gates, ups, results = refs[0:4], refs[4:8], refs[8:12]
    units = gates[0].shape[1]
    for gate, up, result in zip(gates, ups, results):
        result[:, :units, :] = gate[...]
        result[:, units:, :] = up[...]


def back_kernel(head, *refs):
    blocks, mats, own = refs[0:6], refs[6:9], refs[9]
    for e in range(LOCAL):
        rows = blocks[e].shape[0]
        total = dot_nn(blocks[e][...], mats[0][e])
        for q in range(1, 3):
            total = total + dot_nn(blocks[2 * q + e][...], mats[q][e])
        own[pl.ds(e * rows, rows), :] = total


def tangle_kernel(head, own, low, high, mat, send_ref, wide, total):
    rows = own.shape[0] // 2
    sources = rows // CAP
    half = own.shape[1] // 2
    lanes = wide[0].shape[1]
    for e, block in ((0, low), (1, high)):
        total[...] = own[pl.ds(e * rows, rows), :] + dot_nn(block[...], mat[e])
        for c in range(CAP):
            for part in range(2):
                for p in range(half // lanes):
                    col = part * half + p * lanes
                    at = pl.ds(part * SLOTS + e * CAP + c, sources, stride=GROUP)
                    wide[p][at, :] = total[c * sources : (c + 1) * sources, col : col + lanes]
    for p in range(half // lanes):
        send_ref[:, p * lanes : (p + 1) * lanes] = wide[p][...].astype(BF)


def weight_kernel(head, *refs):
    blocks, low, high, results = refs[0:8], refs[8], refs[9], refs[10:]
    width = blocks[0].shape[1]
    units = results[0].shape[1]
    offsets = (0, 3, 1, 2)
    for q in range(4):
        col = pl.multiple_of(((head[0] + offsets[q]) % 4) * width, width)
        for e, left in ((0, low), (1, high)):
            part = dot_tn(left[...], blocks[2 * q + e][...]).astype(BF)
            for i, result in enumerate(results):
                result[e, :, pl.ds(col, width)] = part[i * units : (i + 1) * units, :]


def round_ring(low, high):
    right_low = turned(low, 1)
    left_high = turned(high, -1)
    right_high = turned(high, 1)
    left_low = turned(low, -1)
    far_low = turned(right_low, 1)
    far_high = turned(left_high, -1)
    return [low, high, right_low, right_high, left_low, left_high, far_low, far_high]


def join_kernel(head, *refs):
    parts, result = refs[:4], refs[4]
    width = parts[0].shape[1]
    for part, offset in zip(parts, (0, 3, 1, 2)):
        col = pl.multiple_of(((head[0] + offset) % 4) * width, width)
        result[:, pl.ds(col, width)] = part[...]


def exchange(send, count):
    half = send.shape[1]
    return lax.all_to_all(
        send.reshape(count, GROUP, half), "ctx", split_axis=0, concat_axis=0, tiled=True
    ).reshape(count * GROUP, half)


def dispatch(send, head, count, lanes):
    half = send.shape[1]
    recv = exchange(send, count)
    low, high = call(
        untangle_kernel,
        head,
        [full(recv)],
        [out((count * CAP, 2 * half), BF), out((count * CAP, 2 * half), BF)],
        [[pltpu.VMEM((count * GROUP, lanes), F32) for _ in range(half // lanes)]],
    )
    return round_ring(low, high)


def attention_kernel(head, query, out_ref, grad, kv3, kv2, kv1, kv0, query_seg, key_seg, *refs):
    grad_query, t3, t2, t1, t0, window, key_sum, value_sum = refs
    rows = query.shape[0]
    span = window.shape[0]
    scale = HD ** (-0.5)
    for at, block in enumerate((kv3, kv2, kv1, kv0)):
        window[at * rows : (at + 1) * rows, :] = block[...]
    key_sum[...] = jnp.zeros_like(key_sum)
    value_sum[...] = jnp.zeros_like(value_sum)
    query_at = lax.broadcasted_iota(jnp.int32, (rows, span), 0) + (span - rows)
    key_at = lax.broadcasted_iota(jnp.int32, (rows, span), 1)
    visible = (key_at <= query_at) & (query_seg[...] == key_seg[...])

    def one_head(g, carry):
        lanes = pl.ds(pl.multiple_of(g * HD, HD), HD)
        keys, values = window[:, :HD], window[:, HD:]
        q, dout = query[:, lanes], grad[:, lanes]
        scores = dot_nt(q, keys) * scale
        peak = jnp.max(jnp.where(visible, scores, -jnp.inf), axis=1, keepdims=True)
        weights = jnp.exp(jnp.where(visible, scores - peak, -jnp.inf))
        probs = weights / jnp.sum(weights, axis=1, keepdims=True)
        delta = jnp.sum(dout.astype(F32) * out_ref[:, lanes].astype(F32), axis=1, keepdims=True)
        score_grad = (probs * (dot_nt(dout, values) - delta)).astype(BF)
        grad_query[:, lanes] = (scale * dot_nn(score_grad, keys)).astype(BF)
        key_sum[...] += dot_tn(score_grad, q)
        value_sum[...] += dot_tn(probs.astype(BF), dout)
        return carry

    lax.fori_loop(0, query.shape[1] // HD, one_head, 0)
    for at, ref in enumerate((t3, t2, t1, t0)):
        part = pl.ds(at * rows, rows)
        ref[:, :HD] = scale * key_sum[part, :]
        ref[:, HD:] = value_sum[part, :]


def attention(head, query_rows, kv_blocks, attn_out, grad_attn, segment_ids):
    rows = query_rows.shape[0]
    window = (REACH + 1) * rows
    at = lax.axis_index("ctx") * rows
    padded = jnp.concatenate([jnp.full((REACH * rows,), -1, jnp.int32), segment_ids])
    key_seg = lax.dynamic_slice_in_dim(padded, at, window, 0).reshape(1, window)
    query_seg = lax.dynamic_slice_in_dim(segment_ids, at, rows, 0).reshape(rows, 1)
    return call(
        attention_kernel,
        head,
        [full(query_rows), full(attn_out), full(grad_attn)]
        + [full(b) for b in kv_blocks]
        + [full(query_seg), full(key_seg)],
        [out(query_rows.shape, BF)] + [out((rows, 2 * HD), F32) for _ in range(REACH + 1)],
        [
            pltpu.VMEM((window, 2 * HD), BF),
            pltpu.VMEM((window, HD), F32),
            pltpu.VMEM((window, HD), F32),
        ],
    )


def body(
    tokens,
    grad_out,
    expert_ids,
    gate_probs,
    w_gate,
    w_up,
    w_down,
    query_rows,
    key_rows,
    value_rows,
    attn_out,
    grad_attn,
    segment_ids,
):
    tok_count, width = tokens.shape
    count = lax.axis_size("ctx")
    quarter = width // 4
    half = quarter // 2
    lanes = min(half, 128)
    hidden_local = w_gate.shape[1]
    head = lax.axis_index("head").astype(jnp.int32).reshape(1)
    experts = count * LOCAL
    slots = count * GROUP
    rows = count * CAP
    kv_width = key_rows.shape[1]

    kv = jnp.concatenate([key_rows, value_rows], axis=1)
    kv_blocks = [passed_along(kv, "ctx", distance) for distance in range(REACH, 0, -1)]

    send_rows, pick, scaled = call(
        route_kernel,
        head,
        [
            full(expert_ids.T),
            full(gate_probs.T),
            (tokens, column_block(tokens.shape, 0)),
        ],
        [out((slots, half), BF), out((slots, 2 * tok_count), BF), out((slots, 2 * tok_count), BF)],
        [pltpu.VMEM((experts, tok_count), F32), pltpu.VMEM((experts, tok_count), F32)],
    )
    (send_grads,) = call(
        select_kernel,
        head,
        [full(scaled), (grad_out, column_block(grad_out.shape, 0))],
        [out((slots, half), BF)],
    )
    row_blocks = dispatch(send_rows, head, count, lanes)
    grad_blocks = dispatch(send_grads, head, count, lanes)

    gate_at = lambda offset: (w_gate, column_block(w_gate.shape, offset))
    up_at = lambda offset: (w_up, column_block(w_up.shape, offset))
    down_at = lambda offset: (w_down, column_block(w_down.shape, offset))
    order = (0, 3, 1, 2)
    mat_shape = (LOCAL, 2 * hidden_local, quarter)
    mats = call(
        columns_kernel,
        head,
        [gate_at(o) for o in (0, 1, 3, 2)] + [up_at(o) for o in (0, 1, 3, 2)],
        [out(mat_shape, BF) for _ in range(4)],
    )
    mats = [mats[0]] + [turned(m, distance) for m, distance in zip(mats[1:], (1, 3, 2))]
    act, slope, hidden_low, hidden_high = call(
        pre_kernel,
        head,
        [full(b) for b in row_blocks] + [gate_at(o) for o in order] + [up_at(o) for o in order],
        [
            out((2 * rows, hidden_local), F32),
            out((2 * rows, hidden_local), F32),
            out((rows, hidden_local), BF),
            out((rows, hidden_local), BF),
        ],
    )
    (got_near,) = call(
        near_kernel,
        head,
        [full(b) for b in grad_blocks[:6]] + [down_at(o) for o in order[:3]],
        [out((2 * rows, hidden_local), F32)],
    )
    gu_low, gu_high = call(
        grad_kernel,
        head,
        [full(b) for b in grad_blocks[6:]]
        + [down_at(2), full(got_near), full(act), full(slope)],
        [out((rows, 2 * hidden_local), BF), out((rows, 2 * hidden_local), BF)],
    )
    gu_blocks = round_ring(gu_low, gu_high)
    (own,) = call(
        back_kernel,
        head,
        [full(b) for b in gu_blocks[:6]] + [full(m) for m in mats[:3]],
        [out((2 * rows, quarter), F32)],
    )
    (send_back,) = call(
        tangle_kernel,
        head,
        [full(own), full(gu_blocks[6]), full(gu_blocks[7]), full(mats[3])],
        [out((slots, half), BF)],
        [
            [pltpu.VMEM((slots, lanes), F32) for _ in range(half // lanes)],
            pltpu.VMEM((rows, quarter), F32),
        ],
    )
    returned = exchange(send_back, count)
    summed = dot_tn(pick, returned)
    token_part = jnp.concatenate([summed[:tok_count], summed[tok_count:]], axis=1).astype(BF)
    parts = [token_part] + [turned(token_part, distance) for distance in (1, 3, 2)]
    (grad_tokens,) = call(join_kernel, head, [full(p) for p in parts], [out(tokens.shape, BF)])

    weight_out = out(w_gate.shape, BF)
    grad_gate, grad_up = call(
        weight_kernel,
        head,
        [full(b) for b in row_blocks] + [full(gu_low), full(gu_high)],
        [weight_out, weight_out],
    )
    (grad_down,) = call(
        weight_kernel,
        head,
        [full(b) for b in grad_blocks] + [full(hidden_low), full(hidden_high)],
        [weight_out],
    )

    grad_query, *terms = attention(
        head, query_rows, kv_blocks + [kv], attn_out, grad_attn, segment_ids
    )
    total = terms[REACH]
    for distance in range(1, REACH + 1):
        total = total + passed_along(terms[REACH - distance], "ctx", -distance)
    total = total.astype(BF)
    return (
        grad_tokens,
        grad_gate,
        grad_up,
        grad_down,
        grad_query,
        total[:, :kv_width],
        total[:, kv_width:],
    )


def solution(mesh):
    placed = (
        P("ctx", None),
        P("ctx", None),
        P("ctx", None),
        P("ctx", None),
        P("ctx", "head", None),
        P("ctx", "head", None),
        P("ctx", "head", None),
        P("ctx", "head"),
        P("ctx", "head"),
        P("ctx", "head"),
        P("ctx", "head"),
        P("ctx", "head"),
        P(),
    )
    return jax.shard_map(
        body,
        mesh=mesh,
        in_specs=placed,
        out_specs=(
            P("ctx", None),
            P("ctx", "head", None),
            P("ctx", "head", None),
            P("ctx", "head", None),
            P("ctx", "head"),
            P("ctx", "head"),
            P("ctx", "head"),
        ),
        check_vma=False,
    )
```
